32 devices in a mesh: row: 8 (over z, x), col: 4 (over y, core).
Axes of the slice: x: 2, y: 2, z: 4, core: 2. Of those that a mesh axis runs over, the one named last changes fastest.
Arguments:
- vectors: float32 [8, 4096], P(None, ('row', 'col')), may hold values from -6 to 6
- values: float32 [512, 16384], P('row', 'col'), may hold values from -1 to 1
- block_rows: int32 [8, 256], P('row', 'col'), may hold values from 0 to 7
- block_cols: int32 [8, 256], P('row', 'col'), may hold values from 0 to 15
- counts: int32 [8, 4], P('row', 'col'), may hold values from 16 to 64, as said below
Outputs:
- product: float32 [8, 4096], P(None, ('row', 'col'))
The draws below stay inside these ranges and needn't reach their ends.
Inputs may be any that keep to these rules, and one draw needn't show every extreme that they name: counts[r, c] slots of tile (r, c) hold blocks, the others are unused; some tile uses all 64 slots.
All inputs are finite; a program needn't handle non-finite values.
Results may differ from the reference program's by a relative error of at most 0.0003.
Values sent between devices are 32-bit elements; how exact they have to be, the bound alone decides.
No kernel may reach another device: no remote copies, remote signals or barrier semaphores. Data moves between devices by JAX's collectives and lax.ppermute only.
A program may use at most 64 MiB of HBM per device.

```python
import jax
import jax.numpy as jnp
from jax import lax

PIECE = 128
NB = 64
BLK = 64
NVEC = 8
ROWBLK = 8
COLBLK = 16
NSTATES = 4096
N_ROW = 8
N_COL = 4


def draw_counts(key, part):
    first, second = jax.random.split(jax.random.fold_in(key, 7))
    base = jax.random.randint(first, (N_ROW * N_COL,), NB // 4, NB + 1)
    where = jax.random.randint(second, (), 0, N_ROW * N_COL)
    base = jnp.where(jnp.arange(N_ROW * N_COL) == where, NB, base)
    return base.reshape(N_ROW, N_COL).astype(jnp.int32)


def with_ends(result, key, least, top_value):
    longest = result.shape.index(max(result.shape))
    spots = []
    for shift in (0, 1):
        where = [jax.random.randint(jax.random.fold_in(key, axis), (), 0, length) for axis, length in enumerate(result.shape)]
        where[longest] = (where[longest] + shift) % result.shape[longest]
        spots.append(tuple(where))
    return result.at[spots[0]].set(least).at[spots[1]].set(top_value)


def shard_levels(key, shape, shards, smallest, high):
    def one(axis_at, parts):
        steps = jax.random.uniform(jax.random.fold_in(jax.random.fold_in(key, 6), axis_at), (parts,), jnp.float32, smallest / len(shards), high / len(shards))
        return jnp.repeat(jnp.exp(steps), shape[axis_at] // parts).reshape((-1,) + (1,) * (len(shape) - axis_at - 1))

    factor_of = one(*shards[0])
    for cut in shards[1:]:
        factor_of = factor_of * one(*cut)
    return factor_of


def gaussian(own_key, dims, scale, most, cuts=(), kind=jnp.bfloat16):
    gain = shard_levels(own_key, dims, cuts, -0.22, 0.18) if cuts else 1.0
    array = jax.random.normal(own_key, dims, jnp.float32) * scale * gain
    return jnp.minimum(jnp.maximum(array, -most), most).astype(kind)


def setup_inputs(seed: int = 0) -> dict:
    keys = jax.random.split(jax.random.key(seed), 6)
    vectors = gaussian(keys[0], (NVEC, NSTATES), 1.0, 6.0, ((1, 32),), jnp.float32)
    values = gaussian(keys[1], (N_ROW * NB, N_COL * BLK * BLK), 0.125, 1.0, ((0, 8), (1, 4)), jnp.float32)
    block_rows = with_ends(jax.random.randint(keys[2], (N_ROW, N_COL * NB), 0, ROWBLK), jax.random.fold_in(keys[2], 1), 0, ROWBLK - 1).astype(jnp.int32)
    block_cols = with_ends(jax.random.randint(keys[3], (N_ROW, N_COL * NB), 0, COLBLK), jax.random.fold_in(keys[3], 1), 0, COLBLK - 1).astype(jnp.int32)
    counts = draw_counts(jax.random.fold_in(keys[5], 71), 0)
    return {"vectors": vectors, "values": values, "block_rows": block_rows, "block_cols": block_cols, "counts": counts}


def tile_terms(blocks, rows, cols, count, row_seg, col_seg):
    highest = lax.Precision.HIGHEST
    slots = blocks.shape[0]
    nvec = row_seg.shape[0]
    row_blocks = row_seg.shape[1] // blocks.shape[1]
    col_blocks = col_seg.shape[1] // blocks.shape[1]
    width = blocks.shape[1]
    live = (jnp.arange(slots, dtype=jnp.int32) < count).astype(jnp.float32)
    row_hits = (rows[:, None] == jnp.arange(row_blocks, dtype=jnp.int32)[None, :]).astype(jnp.float32) * live[:, None]
    col_hits = (cols[:, None] == jnp.arange(col_blocks, dtype=jnp.int32)[None, :]).astype(jnp.float32) * live[:, None]
    row_parts = row_seg.reshape(nvec, row_blocks, width)
    col_parts = col_seg.reshape(nvec, col_blocks, width)
    col_pick = jnp.take(col_parts, cols, axis=1)
    row_pick = jnp.take(row_parts, rows, axis=1)
    plain = jnp.einsum("kij,vkj->vki", blocks, col_pick, precision=highest)
    turned = jnp.einsum("kji,vkj->vki", blocks, row_pick, precision=highest)
    plain_part = jnp.einsum("kb,vki->vbi", row_hits, plain, precision=highest).reshape(nvec, row_blocks * width)
    turned_part = jnp.einsum("kb,vki->vbi", col_hits, turned, precision=highest).reshape(nvec, col_blocks * width)
    return plain_part, turned_part


def reference(vectors, values, block_rows, block_cols, counts):
    rows_view = vectors.reshape(NVEC, N_ROW, N_COL * PIECE)
    grid = vectors.reshape(NVEC, N_ROW, N_COL, PIECE)
    col_view = jnp.transpose(grid, (2, 0, 1, 3)).reshape(N_COL, NVEC, N_ROW * PIECE)
    tiles = values.reshape(N_ROW, NB, N_COL, BLK, BLK)

    def one_row(index):
        row_seg = lax.dynamic_index_in_dim(rows_view, index, 1, False)
        row_tiles = jnp.moveaxis(lax.dynamic_index_in_dim(tiles, index, 0, False), 1, 0)
        rows_here = lax.dynamic_index_in_dim(block_rows, index, 0, False).reshape(N_COL, NB)
        cols_here = lax.dynamic_index_in_dim(block_cols, index, 0, False).reshape(N_COL, NB)
        count_here = lax.dynamic_index_in_dim(counts, index, 0, False)
        plain, turned = jax.vmap(tile_terms, in_axes=(0, 0, 0, 0, None, 0))(
            row_tiles, rows_here, cols_here, count_here, row_seg, col_view)
        return jnp.sum(plain, axis=0), turned

    plain_all, turned_all = lax.map(one_row, jnp.arange(N_ROW, dtype=jnp.int32))
    plain_full = jnp.transpose(plain_all, (1, 0, 2)).reshape(NVEC, NSTATES)
    turned_sum = jnp.sum(turned_all, axis=0).reshape(N_COL, NVEC, N_ROW, PIECE)
    turned_full = jnp.transpose(turned_sum, (1, 2, 0, 3)).reshape(NVEC, NSTATES)
    return plain_full + turned_full
```

```python
import functools
import math

import jax
import jax.numpy as jnp
from jax import lax
from jax.experimental import pallas as pl
from jax.experimental.pallas import tpu as pltpu
from jax.sharding import PartitionSpec as P

LANES = 128
SUB = 8
DENSE_LIMIT = 4 << 20
f32, bf16 = jnp.float32, jnp.bfloat16
VMEM = pl.BlockSpec(memory_space=pltpu.VMEM)
SMEM = pl.BlockSpec(memory_space=pltpu.SMEM)
NT = (((1,), (1,)), ((), ()))


def tile_terms(blocks, rows, cols, count, row_seg, col_seg):
    highest = lax.Precision.HIGHEST
    slots = blocks.shape[0]
    nvec = row_seg.shape[0]
    row_blocks = row_seg.shape[1] // blocks.shape[1]
    col_blocks = col_seg.shape[1] // blocks.shape[1]
    width = blocks.shape[1]
    live = (jnp.arange(slots, dtype=jnp.int32) < count).astype(jnp.float32)
    row_hits = (rows[:, None] == jnp.arange(row_blocks, dtype=jnp.int32)[None, :]).astype(jnp.float32) * live[:, None]
    col_hits = (cols[:, None] == jnp.arange(col_blocks, dtype=jnp.int32)[None, :]).astype(jnp.float32) * live[:, None]
    row_parts = row_seg.reshape(nvec, row_blocks, width)
    col_parts = col_seg.reshape(nvec, col_blocks, width)
    col_pick = jnp.take(col_parts, cols, axis=1)
    row_pick = jnp.take(row_parts, rows, axis=1)
    plain = jnp.einsum("kij,vkj->vki", blocks, col_pick, precision=highest)
    turned = jnp.einsum("kji,vkj->vki", blocks, row_pick, precision=highest)
    plain_part = jnp.einsum("kb,vki->vbi", row_hits, plain, precision=highest).reshape(nvec, row_blocks * width)
    turned_part = jnp.einsum("kb,vki->vbi", col_hits, turned, precision=highest).reshape(nvec, col_blocks * width)
    return plain_part, turned_part


def by_blocks(blk, vectors, values, block_rows, block_cols, counts):
    row_seg = lax.all_gather(vectors, "col", axis=1, tiled=True)
    col_seg = lax.all_gather(vectors, "row", axis=1, tiled=True)
    blocks = values.reshape(values.shape[0], blk, blk)
    plain, turned = tile_terms(blocks, block_rows[0], block_cols[0], counts[0, 0], row_seg, col_seg)
    plain = lax.psum_scatter(plain, "col", scatter_dimension=1, tiled=True)
    turned = lax.psum_scatter(turned, "row", scatter_dimension=1, tiled=True)
    return plain + turned


def build_kernel(blk, row_bits, col_bits, values, rows, cols, count, hi, lo, acc):
    r, c = lax.axis_index("row"), lax.axis_index("col")
    half = blk // 2
    steps = half // SUB
    group = half * SUB
    acc[...] = jnp.zeros_like(acc)

    def add_slot(k, carry):
        br = rows[0, k] ^ (c * 2)
        bc = cols[0, k] ^ (r * 2)
        first = (k // SUB) * group + k % SUB
        for q in range(steps):
            piece = values[pl.ds(first + q * SUB * SUB, SUB, stride=SUB), :]
            at = pl.multiple_of(br * half + q * SUB, SUB)
            acc[bc, pl.ds(at, SUB), :] += piece
        return carry

    lax.fori_loop(0, count[0, 0], add_slot, 0)
    for b in range(acc.shape[0]):
        dense = acc[b]
        top = dense.astype(bf16)
        hi[b] = top
        lo[b] = (dense - top.astype(f32)).astype(bf16)


def build(blk, nbr, nbc, values, block_rows, block_cols, counts):
    slots = values.shape[0]
    half = blk // 2
    view = values.reshape(slots // SUB, SUB, half, LANES).transpose(0, 2, 1, 3).reshape(slots * half, LANES)
    shape = (nbc, nbr * half, LANES)
    return pl.pallas_call(
        functools.partial(build_kernel, blk, 0, 0),
        out_shape=[jax.ShapeDtypeStruct(shape, bf16)] * 2,
        in_specs=[VMEM, SMEM, SMEM, SMEM],
        out_specs=[VMEM, VMEM],
        scratch_shapes=[pltpu.VMEM(shape, f32)],
        compiler_params=pltpu.CompilerParams(vmem_limit_bytes=12 << 20),
        cost_estimate=pl.CostEstimate(flops=1 << 20, bytes_accessed=6 << 20, transcendentals=0),
        name="build",
    )(view, block_rows, block_cols, counts)


def split(x):
    top = x.astype(bf16).astype(f32)
    return jnp.concatenate([top, x - top], 0)


def fold():
    src = lax.broadcasted_iota(jnp.int32, (LANES, LANES), 0)
    dst = lax.broadcasted_iota(jnp.int32, (LANES, LANES), 1)
    half = LANES // 4
    want = ((dst // half) % 2) * (LANES // 2) + 2 * (dst % half) + dst // (LANES // 2)
    return (src == want).astype(f32).astype(bf16)


def low(rows):
    return lax.broadcasted_iota(jnp.int32, (rows, LANES), 1) < LANES // 2


def swap(x):
    return pltpu.roll(x, LANES // 2, 1)


def wide(ref, q):
    return jnp.concatenate([ref[2 * q], ref[2 * q + 1]], 1)


def load(refs):
    out = []
    for ref in refs:
        if len(ref.shape) == 2:
            out.append(ref[...])
        else:
            out += [ref[i] for i in range(ref.shape[0])]
    return out


def turned_kernel(nx, nout, *refs):
    xs, (hi, lo), outs = load(refs[:nx]), refs[nx : nx + 2], refs[nx + 2 :]
    nv = xs[0].shape[0]
    folded = jnp.dot(jnp.concatenate([split(x) for x in xs], 0).astype(bf16), fold(), preferred_element_type=f32)
    m = low(2 * nv)
    even, odd = [], []
    for g in range(len(xs) // 2):
        a, b = folded[4 * nv * g : 4 * nv * g + 2 * nv], folded[4 * nv * g + 2 * nv : 4 * nv * g + 4 * nv]
        even.append(jnp.where(m, a, swap(b)))
        odd.append(jnp.where(m, swap(a), b))
    left = jnp.concatenate([jnp.concatenate(even, 1), jnp.concatenate(odd, 1)], 0).astype(bf16)
    m = low(nv)
    q = 0
    for out in outs:
        for i in range(out.shape[0]):
            t = jnp.dot(left, wide(hi, q), preferred_element_type=f32) + jnp.dot(left, wide(lo, q), preferred_element_type=f32)
            t0, t1 = t[:nv] + t[nv : 2 * nv], t[2 * nv : 3 * nv] + t[3 * nv :]
            out[i] = jnp.where(m, t0[:, :LANES] + swap(t1[:, :LANES]), swap(t0[:, LANES:]) + t1[:, LANES:])
            q += 1


def plain_kernel(nx, nout, *refs):
    xs, (hi, lo), outs = load(refs[:nx]), refs[nx : nx + 2], refs[nx + 2 :]
    nv = xs[0].shape[0]
    m = low(2 * nv)
    total = None
    for q, x in enumerate(xs):
        s = split(x)
        r = swap(s)
        first = jnp.concatenate([jnp.where(m, s, 0.0), jnp.where(m, 0.0, r)], 0)
        second = jnp.concatenate([jnp.where(m, r, 0.0), jnp.where(m, 0.0, s)], 0)
        left = jnp.concatenate([first, second], 1).astype(bf16)
        t = lax.dot_general(left, wide(hi, q), NT, preferred_element_type=f32)
        t += lax.dot_general(left, wide(lo, q), NT, preferred_element_type=f32)
        total = t if total is None else total + t
    z0, z1 = total[:nv] + total[nv : 2 * nv], total[2 * nv : 3 * nv] + total[3 * nv :]
    m = low(nv)
    parts = []
    for g in range(z0.shape[1] // LANES):
        a, b = z0[:, LANES * g : LANES * (g + 1)], z1[:, LANES * g : LANES * (g + 1)]
        parts += [split(jnp.where(m, a, swap(b))), split(jnp.where(m, swap(a), b))]
    back = lax.dot_general(jnp.concatenate(parts, 0).astype(bf16), fold(), NT, preferred_element_type=f32)
    k = 0
    for out in outs:
        for i in range(out.shape[0]):
            out[i] = back[2 * nv * k : 2 * nv * k + nv] + back[2 * nv * k + nv : 2 * nv * (k + 1)]
            k += 1


def call(kernel, name, xs, hi, lo, outs):
    nv = xs[0].shape[-2]
    return pl.pallas_call(
        functools.partial(kernel, len(xs), len(outs)),
        out_shape=[jax.ShapeDtypeStruct((n, nv, LANES), f32) for n in outs],
        in_specs=[VMEM] * (len(xs) + 2),
        out_specs=[VMEM] * len(outs),
        compiler_params=pltpu.CompilerParams(vmem_limit_bytes=12 << 20),
        cost_estimate=pl.CostEstimate(flops=1 << 26, bytes_accessed=2 << 20, transcendentals=0),
        name=name,
    )(*xs, hi, lo)


def turned_of(xs, hi, lo, outs):
    return call(turned_kernel, "turned", xs, hi, lo, outs)


def plain_of(xs, hi, lo, outs):
    return call(plain_kernel, "plain", xs, hi, lo, outs)


def trade(x, axis, step):
    n = lax.axis_size(axis)
    return lax.ppermute(x, axis, [(i, i ^ step) for i in range(n)])

def exchange(v, hi, lo):
    x1 = trade(v, "row", 1)
    y = [v] + [trade(v, "col", k) for k in (1, 2, 3)]
    t0, t1 = turned_of(y, hi, lo, (4, 4))
    s1 = jnp.stack([v, x1])
    z1 = trade(s1, "row", 2)
    s2 = jnp.concatenate([s1, z1])
    z2 = trade(s2, "row", 4)
    p = plain_of([s2, z2], hi, lo, (1, 1, 1, 1))
    out = p[0][0]
    u = t0 + trade(t1, "row", 4)
    u = u[:2] + trade(u[2:], "row", 2)
    for k in (1, 2, 3):
        out = out + trade(p[k][0], "col", k)
    return out + u[0] + trade(u[1], "row", 1)


def solution(mesh):
    sizes = mesh.shape

    def per_device(vectors, values, block_rows, block_cols, counts):
        blk = math.isqrt(values.shape[1])
        piece = vectors.shape[1]
        nbr, nbc = sizes["col"] * piece // blk, sizes["row"] * piece // blk
        fits = nbr * nbc * blk * blk * 4 <= DENSE_LIMIT
        square = sizes["row"] == 8 and sizes["col"] == 4
        if not (fits and square and piece == LANES and 2 * blk == LANES and values.shape[0] % SUB == 0):
            return by_blocks(blk, vectors, values, block_rows, block_cols, counts)
        hi, lo = build(blk, nbr, nbc, values, block_rows, block_cols, counts)
        return exchange(vectors, hi, lo)

    spec = P("row", "col")
    return jax.shard_map(
        per_device,
        mesh=mesh,
        in_specs=(P(None, ("row", "col")), spec, spec, spec, spec),
        out_specs=P(None, ("row", "col")),
        check_vma=False,
    )
```

```python
import functools
import math

import jax
import jax.numpy as jnp
from jax import lax
from jax.experimental import pallas as pl
from jax.experimental.pallas import tpu as pltpu
from jax.sharding import PartitionSpec as P

LANES = 128
SUB = 8
DENSE_LIMIT = 4 << 20
f32, bf16 = jnp.float32, jnp.bfloat16
VMEM = pl.BlockSpec(memory_space=pltpu.VMEM)
SMEM = pl.BlockSpec(memory_space=pltpu.SMEM)
NT = (((1,), (1,)), ((), ()))


def tile_terms(blocks, rows, cols, count, row_seg, col_seg):
    highest = lax.Precision.HIGHEST
    slots = blocks.shape[0]
    nvec = row_seg.shape[0]
    row_blocks = row_seg.shape[1] // blocks.shape[1]
    col_blocks = col_seg.shape[1] // blocks.shape[1]
    width = blocks.shape[1]
    live = (jnp.arange(slots, dtype=jnp.int32) < count).astype(jnp.float32)
    row_hits = (rows[:, None] == jnp.arange(row_blocks, dtype=jnp.int32)[None, :]).astype(jnp.float32) * live[:, None]
    col_hits = (cols[:, None] == jnp.arange(col_blocks, dtype=jnp.int32)[None, :]).astype(jnp.float32) * live[:, None]
    row_parts = row_seg.reshape(nvec, row_blocks, width)
    col_parts = col_seg.reshape(nvec, col_blocks, width)
    col_pick = jnp.take(col_parts, cols, axis=1)
    row_pick = jnp.take(row_parts, rows, axis=1)
    plain = jnp.einsum("kij,vkj->vki", blocks, col_pick, precision=highest)
    turned = jnp.einsum("kji,vkj->vki", blocks, row_pick, precision=highest)
    plain_part = jnp.einsum("kb,vki->vbi", row_hits, plain, precision=highest).reshape(nvec, row_blocks * width)
    turned_part = jnp.einsum("kb,vki->vbi", col_hits, turned, precision=highest).reshape(nvec, col_blocks * width)
    return plain_part, turned_part


def by_blocks(blk, vectors, values, block_rows, block_cols, counts):
    row_seg = lax.all_gather(vectors, "col", axis=1, tiled=True)
    col_seg = lax.all_gather(vectors, "row", axis=1, tiled=True)
    blocks = values.reshape(values.shape[0], blk, blk)
    plain, turned = tile_terms(blocks, block_rows[0], block_cols[0], counts[0, 0], row_seg, col_seg)
    plain = lax.psum_scatter(plain, "col", scatter_dimension=1, tiled=True)
    turned = lax.psum_scatter(turned, "row", scatter_dimension=1, tiled=True)
    return plain + turned


def build_kernel(blk, vectors, values, rows, cols, count, own, hi, lo, acc, held, row_of, col_of, sems):
    r, c = lax.axis_index("row"), lax.axis_index("col")
    half = blk // 2
    steps = half // SUB
    group = half * SUB
    groups = held.shape[0] // group
    small = [
        pltpu.make_async_copy(src, dst, sems.at[groups + i])
        for i, (src, dst) in enumerate(((rows, row_of), (cols, col_of), (vectors, own)))
    ]
    large = [
        pltpu.make_async_copy(values.at[pl.ds(g * group, group)], held.at[pl.ds(g * group, group)], sems.at[g])
        for g in range(groups)
    ]
    for copy in small + large:
        copy.start()
    acc[...] = jnp.zeros_like(acc)
    for copy in small:
        copy.wait()
    used = jnp.broadcast_to(count[...], (SUB, LANES))

    def add_slot(k, first):
        br = row_of[0, k] ^ (c * 2)
        bc = col_of[0, k] ^ (r * 2)
        for q in range(steps):
            piece = jnp.where(used > k, held[pl.ds(first + q * SUB * SUB, SUB, stride=SUB), :], 0.0)
            at = pl.multiple_of(br * half + q * SUB, SUB)
            acc[bc, pl.ds(at, SUB), :] += piece

    for g in range(groups):
        large[g].wait()
        for s in range(SUB):
            add_slot(g * SUB + s, g * group + s)
    for b in range(acc.shape[0]):
        dense = acc[b]
        top = dense.astype(bf16)
        hi[b] = top
        lo[b] = (dense - top.astype(f32)).astype(bf16)


def build(blk, nbr, nbc, vectors, values, block_rows, block_cols, counts):
    slots = values.shape[0]
    half = blk // 2
    view = values.reshape(slots // SUB, SUB, half, LANES).transpose(0, 2, 1, 3).reshape(slots * half, LANES)
    shape = (nbc, nbr * half, LANES)
    hbm = pl.BlockSpec(memory_space=pltpu.HBM)
    vectors, view, block_rows, block_cols = (
        pltpu.with_memory_space_constraint(x, pltpu.HBM) for x in (vectors, view, block_rows, block_cols)
    )
    return pl.pallas_call(
        functools.partial(build_kernel, blk),
        out_shape=[jax.ShapeDtypeStruct(vectors.shape, f32)] + [jax.ShapeDtypeStruct(shape, bf16)] * 2,
        in_specs=[hbm] * 4 + [VMEM],
        out_specs=[VMEM] * 3,
        scratch_shapes=[
            pltpu.VMEM(shape, f32),
            pltpu.VMEM(view.shape, f32),
            pltpu.SMEM(block_rows.shape, jnp.int32),
            pltpu.SMEM(block_cols.shape, jnp.int32),
            pltpu.SemaphoreType.DMA((slots // SUB + 3,)),
        ],
        compiler_params=pltpu.CompilerParams(vmem_limit_bytes=12 << 20),
        cost_estimate=pl.CostEstimate(flops=1 << 20, bytes_accessed=6 << 20, transcendentals=0),
        name="build",
    )(vectors, view, block_rows, block_cols, counts)


def split(x):
    top = x.astype(bf16).astype(f32)
    return jnp.concatenate([top, x - top], 0)


def fold():
    src = lax.broadcasted_iota(jnp.int32, (LANES, LANES), 0)
    dst = lax.broadcasted_iota(jnp.int32, (LANES, LANES), 1)
    half = LANES // 4
    want = ((dst // half) % 2) * (LANES // 2) + 2 * (dst % half) + dst // (LANES // 2)
    return (src == want).astype(f32).astype(bf16)


def low(rows):
    return lax.broadcasted_iota(jnp.int32, (rows, LANES), 1) < LANES // 2


def swap(x):
    return pltpu.roll(x, LANES // 2, 1)


def wide(ref, q):
    return jnp.concatenate([ref[2 * q], ref[2 * q + 1]], 1)


def load(refs):
    out = []
    for ref in refs:
        if len(ref.shape) == 2:
            out.append(ref[...])
        else:
            out += [ref[i] for i in range(ref.shape[0])]
    return out


def turned_kernel(nx, order, *refs):
    xs, (hi, lo), outs = load(refs[:nx]), refs[nx : nx + 2], refs[nx + 2 :]
    xs = [xs[k] for k in order]
    nv = xs[0].shape[0]
    folded = jnp.dot(jnp.concatenate([split(x) for x in xs], 0).astype(bf16), fold(), preferred_element_type=f32)
    m = low(2 * nv)
    even, odd = [], []
    for g in range(len(xs) // 2):
        a, b = folded[4 * nv * g : 4 * nv * g + 2 * nv], folded[4 * nv * g + 2 * nv : 4 * nv * g + 4 * nv]
        even.append(jnp.where(m, a, swap(b)))
        odd.append(jnp.where(m, swap(a), b))
    left = jnp.concatenate([jnp.concatenate(even, 1), jnp.concatenate(odd, 1)], 0).astype(bf16)
    m = low(nv)
    q = 0
    for out in outs:
        for i in range(out.shape[0]):
            t = jnp.dot(left, wide(hi, q), preferred_element_type=f32) + jnp.dot(left, wide(lo, q), preferred_element_type=f32)
            t0, t1 = t[:nv] + t[nv : 2 * nv], t[2 * nv : 3 * nv] + t[3 * nv :]
            out[i] = jnp.where(m, t0[:, :LANES] + swap(t1[:, :LANES]), swap(t0[:, LANES:]) + t1[:, LANES:])
            q += 1


def plain_kernel(nx, order, *refs):
    xs, (hi, lo), outs = load(refs[:nx]), refs[nx : nx + 2], refs[nx + 2 :]
    nv = xs[0].shape[0]
    m = low(2 * nv)
    total = None
    for q, x in enumerate(xs):
        s = split(x)
        r = swap(s)
        first = jnp.concatenate([jnp.where(m, s, 0.0), jnp.where(m, 0.0, r)], 0)
        second = jnp.concatenate([jnp.where(m, r, 0.0), jnp.where(m, 0.0, s)], 0)
        left = jnp.concatenate([first, second], 1).astype(bf16)
        t = lax.dot_general(left, wide(hi, q), NT, preferred_element_type=f32)
        t += lax.dot_general(left, wide(lo, q), NT, preferred_element_type=f32)
        total = t if total is None else total + t
    z0, z1 = total[:nv] + total[nv : 2 * nv], total[2 * nv : 3 * nv] + total[3 * nv :]
    m = low(nv)
    parts = []
    for g in range(z0.shape[1] // LANES):
        a, b = z0[:, LANES * g : LANES * (g + 1)], z1[:, LANES * g : LANES * (g + 1)]
        parts += [split(jnp.where(m, a, swap(b))), split(jnp.where(m, swap(a), b))]
    back = lax.dot_general(jnp.concatenate(parts, 0).astype(bf16), fold(), NT, preferred_element_type=f32)
    at = iter(order)
    for out in outs:
        for i in range(out.shape[0]):
            k = next(at)
            out[i] = back[2 * nv * k : 2 * nv * k + nv] + back[2 * nv * k + nv : 2 * nv * (k + 1)]


def call(kernel, xs, hi, lo, outs, order):
    nv = xs[0].shape[-2]
    return pl.pallas_call(
        functools.partial(kernel, len(xs), order),
        out_shape=[jax.ShapeDtypeStruct((n, nv, LANES), f32) for n in outs],
        in_specs=[VMEM] * (len(xs) + 2),
        out_specs=[VMEM] * len(outs),
        compiler_params=pltpu.CompilerParams(vmem_limit_bytes=12 << 20),
        cost_estimate=pl.CostEstimate(flops=1 << 26, bytes_accessed=2 << 20, transcendentals=0),
    )(*xs, hi, lo)


def turned_of(xs, hi, lo, outs, order):
    return call(turned_kernel, xs, hi, lo, outs, order)


def plain_of(xs, hi, lo, outs, order):
    return call(plain_kernel, xs, hi, lo, outs, order)


def trade(x, axis, step):
    n = lax.axis_size(axis)
    return lax.ppermute(x, axis, [(i, i ^ step) for i in range(n)])


def glue(body, ins, *outs):
    return pl.pallas_call(
        body,
        out_shape=[jax.ShapeDtypeStruct((n,) + ins[0].shape[-2:], f32) for n in outs],
        in_specs=[VMEM] * len(ins),
        out_specs=[VMEM] * len(outs),
        compiler_params=pltpu.CompilerParams(vmem_limit_bytes=1 << 20),
    )(*ins)


def join(*refs):
    out, at = refs[-1], 0
    for x in load(refs[:-1]):
        out[at] = x
        at += 1


def halve(a, b, keep, send):
    n = keep.shape[0]
    for i in range(n):
        keep[i] = a[i] + b[i]
        send[i] = a[n + i] + b[n + i]


def exchange(v, own, hi, lo):
    n1 = trade(v, "col", 1)
    n2 = trade(v, "col", 2)
    n3 = trade(v, "col", 3)
    x1 = trade(v, "row", 1)
    (s1,) = glue(join, [own, x1], 2)
    z1 = trade(s1, "row", 2)
    t0, t1 = turned_of([own, n1, n2, n3], hi, lo, (4, 4), (0, 1, 2, 3))
    far = trade(t1, "row", 4)
    (s2,) = glue(join, [s1, z1], 4)
    z2 = trade(s2, "row", 4)
    u0, u1 = glue(halve, [t0, far], 2, 2)
    mid = trade(u1, "row", 2)
    p0, p1 = plain_of([s2, z2], hi, lo, (2, 2), (0, 1, 3, 2))
    q0 = trade(p1, "col", 3)
    w0, w1 = glue(halve, [u0, mid], 1, 1)
    near = trade(w1, "row", 1)
    g0, g1 = glue(halve, [p0, q0], 1, 1)
    last = trade(g1, "col", 1)
    return (g0 + last + w0 + near)[0]


def solution(mesh):
    sizes = mesh.shape

    def per_device(vectors, values, block_rows, block_cols, counts):
        blk = math.isqrt(values.shape[1])
        piece = vectors.shape[1]
        nbr, nbc = sizes["col"] * piece // blk, sizes["row"] * piece // blk
        fits = nbr * nbc * blk * blk * 4 <= DENSE_LIMIT
        square = sizes["row"] == 8 and sizes["col"] == 4
        if not (fits and square and piece == LANES and 2 * blk == LANES and values.shape[0] % SUB == 0):
            return by_blocks(blk, vectors, values, block_rows, block_cols, counts)
        own, hi, lo = build(blk, nbr, nbc, vectors, values, block_rows, block_cols, counts)
        return exchange(vectors, own, hi, lo)

    spec = P("row", "col")
    return jax.shard_map(
        per_device,
        mesh=mesh,
        in_specs=(P(None, ("row", "col")), spec, spec, spec, spec),
        out_specs=P(None, ("row", "col")),
        check_vma=False,
    )
```

```python
import functools
import math

import jax
import jax.numpy as jnp
from jax import lax
from jax.experimental import pallas as pl
from jax.experimental.pallas import tpu as pltpu
from jax.sharding import PartitionSpec as P

LANES = 128
SUB = 8
DENSE_LIMIT = 4 << 20
f32, bf16 = jnp.float32, jnp.bfloat16
VMEM = pl.BlockSpec(memory_space=pltpu.VMEM)
SMEM = pl.BlockSpec(memory_space=pltpu.SMEM)
NT = (((1,), (1,)), ((), ()))


def tile_terms(blocks, rows, cols, count, row_seg, col_seg):
    highest = lax.Precision.HIGHEST
    slots = blocks.shape[0]
    nvec = row_seg.shape[0]
    row_blocks = row_seg.shape[1] // blocks.shape[1]
    col_blocks = col_seg.shape[1] // blocks.shape[1]
    width = blocks.shape[1]
    live = (jnp.arange(slots, dtype=jnp.int32) < count).astype(jnp.float32)
    row_hits = (rows[:, None] == jnp.arange(row_blocks, dtype=jnp.int32)[None, :]).astype(jnp.float32) * live[:, None]
    col_hits = (cols[:, None] == jnp.arange(col_blocks, dtype=jnp.int32)[None, :]).astype(jnp.float32) * live[:, None]
    row_parts = row_seg.reshape(nvec, row_blocks, width)
    col_parts = col_seg.reshape(nvec, col_blocks, width)
    col_pick = jnp.take(col_parts, cols, axis=1)
    row_pick = jnp.take(row_parts, rows, axis=1)
    plain = jnp.einsum("kij,vkj->vki", blocks, col_pick, precision=highest)
    turned = jnp.einsum("kji,vkj->vki", blocks, row_pick, precision=highest)
    plain_part = jnp.einsum("kb,vki->vbi", row_hits, plain, precision=highest).reshape(nvec, row_blocks * width)
    turned_part = jnp.einsum("kb,vki->vbi", col_hits, turned, precision=highest).reshape(nvec, col_blocks * width)
    return plain_part, turned_part


def by_blocks(blk, vectors, values, block_rows, block_cols, counts):
    row_seg = lax.all_gather(vectors, "col", axis=1, tiled=True)
    col_seg = lax.all_gather(vectors, "row", axis=1, tiled=True)
    blocks = values.reshape(values.shape[0], blk, blk)
    plain, turned = tile_terms(blocks, block_rows[0], block_cols[0], counts[0, 0], row_seg, col_seg)
    plain = lax.psum_scatter(plain, "col", scatter_dimension=1, tiled=True)
    turned = lax.psum_scatter(turned, "row", scatter_dimension=1, tiled=True)
    return plain + turned


def init_kernel(acc):
    acc[...] = jnp.zeros_like(acc)


def build_kernel(blk, values, rows, cols, count, start, hi, lo, acc):
    del start
    r, c = lax.axis_index("row"), lax.axis_index("col")
    half = blk // 2
    steps = half // SUB
    group = half * SUB
    used = jnp.broadcast_to(count[...], (SUB, LANES))
    side = lax.broadcasted_iota(jnp.int32, (SUB, LANES), 1) // blk

    def add_slot(k, first):
        br = rows[0, k] ^ (c * 2)
        bc = cols[0, k] ^ (r * 2)
        q, odd = bc // 2, bc % 2
        keep = (side == odd) & (used > k)
        swapped = jnp.broadcast_to(odd, (SUB, LANES)) == 1
        for s in range(steps):
            two = values[pl.ds(first + s * SUB * SUB, SUB, stride=SUB), :]
            turn = swap(two)
            at = br * blk + 2 * SUB * s
            acc[q, pl.ds(at, SUB, stride=2), :] += jnp.where(keep, jnp.where(swapped, turn, two), 0.0)
            acc[q, pl.ds(at + 1, SUB, stride=2), :] += jnp.where(keep, jnp.where(swapped, two, turn), 0.0)

    for k in range(values.shape[0] // half):
        add_slot(k, k // SUB * group + k % SUB)
    for q in range(acc.shape[0]):
        dense = acc[q]
        top = dense.astype(bf16)
        hi[q] = top
        lo[q] = (dense - top.astype(f32)).astype(bf16)


def build(blk, nbr, nbc, vectors, values, block_rows, block_cols, counts):
    slots = values.shape[0]
    half = blk // 2
    view = values.reshape(slots // SUB, SUB, half, LANES).transpose(0, 2, 1, 3).reshape(slots * half, LANES)
    shape = (nbc // 2, nbr * blk, LANES)
    start = pl.pallas_call(
        init_kernel,
        out_shape=jax.ShapeDtypeStruct(shape, f32),
        out_specs=VMEM,
        compiler_params=pltpu.CompilerParams(vmem_limit_bytes=4 << 20),
        cost_estimate=pl.CostEstimate(flops=1 << 20, bytes_accessed=2 << 20, transcendentals=0),
        name="init",
    )()
    hi, lo, _ = pl.pallas_call(
        functools.partial(build_kernel, blk),
        out_shape=[jax.ShapeDtypeStruct(shape, bf16)] * 2 + [jax.ShapeDtypeStruct(shape, f32)],
        in_specs=[VMEM, SMEM, SMEM, VMEM, VMEM],
        out_specs=[VMEM] * 3,
        input_output_aliases={4: 2},
        compiler_params=pltpu.CompilerParams(vmem_limit_bytes=12 << 20),
        cost_estimate=pl.CostEstimate(flops=1 << 20, bytes_accessed=6 << 20, transcendentals=0),
        name="build",
    )(view, block_rows, block_cols, counts, start)
    return vectors, hi, lo


def split(x):
    top = x.astype(bf16).astype(f32)
    return jnp.concatenate([top, x - top], 0)


def swap(x):
    return pltpu.roll(x, LANES // 2, 1)


def wide(ref, q):
    return jnp.concatenate([ref[q], ref[q + 1]], 1)


def load(refs):
    out = []
    for ref in refs:
        if len(ref.shape) == 2:
            out.append(ref[...])
        else:
            out += [ref[i] for i in range(ref.shape[0])]
    return out


def pieces(refs, names):
    return dict(zip(names, load(refs), strict=True))


def places(refs, names):
    return dict(zip(names, ((ref, i) for ref in refs for i in range(ref.shape[0])), strict=True))


def turned_kernel(nx, take, put, *refs):
    xs, (hi, lo), outs = pieces(refs[:nx], take), refs[nx : nx + 2], places(refs[nx + 2 :], put)
    nv = xs[0].shape[0]
    left = jnp.concatenate([split(xs[k]) for k in range(len(xs))], 1).astype(bf16)
    for q in range(0, len(outs), 2):
        t = jnp.dot(left, wide(hi, q), preferred_element_type=f32) + jnp.dot(left, wide(lo, q), preferred_element_type=f32)
        t = t[:nv] + t[nv:]
        for i in range(2):
            out, at = outs[q + i]
            out[at] = t[:, LANES * i : LANES * (i + 1)]


def plain_kernel(nx, take, put, *refs):
    xs, (hi, lo), outs = pieces(refs[:nx], take), refs[nx : nx + 2], places(refs[nx + 2 :], put)
    nv = xs[0].shape[0]
    total = 0.0
    for q in range(0, len(xs), 2):
        left = jnp.concatenate([split(xs[q]), split(xs[q + 1])], 1).astype(bf16)
        for part in (hi, lo):
            total += lax.dot_general(left, wide(part, q), NT, preferred_element_type=f32)
    total = total[:nv] + total[nv:]
    for k, (out, at) in outs.items():
        out[at] = total[:, LANES * k : LANES * (k + 1)]


def call(kernel, xs, hi, lo, outs, take, put):
    nv = xs[0].shape[-2]
    return pl.pallas_call(
        functools.partial(kernel, len(xs), take, put),
        out_shape=[jax.ShapeDtypeStruct((n, nv, LANES), f32) for n in outs],
        in_specs=[VMEM] * (len(xs) + 2),
        out_specs=[VMEM] * len(outs),
        compiler_params=pltpu.CompilerParams(vmem_limit_bytes=12 << 20),
        cost_estimate=pl.CostEstimate(flops=1 << 26, bytes_accessed=2 << 20, transcendentals=0),
    )(*xs, hi, lo)


def turned_of(xs, hi, lo, outs, take, put):
    return call(turned_kernel, xs, hi, lo, outs, take, put)


def plain_of(xs, hi, lo, outs, take, put):
    return call(plain_kernel, xs, hi, lo, outs, take, put)


def trade(x, axis, step):
    n = lax.axis_size(axis)
    return lax.ppermute(x, axis, [(i, i ^ step) for i in range(n)])


def glue(body, ins, *outs):
    return pl.pallas_call(
        body,
        out_shape=[jax.ShapeDtypeStruct((n,) + ins[0].shape[-2:], f32) for n in outs],
        in_specs=[VMEM] * len(ins),
        out_specs=[VMEM] * len(outs),
        compiler_params=pltpu.CompilerParams(vmem_limit_bytes=1 << 20),
    )(*ins)


def join(*refs):
    out, at = refs[-1], 0
    for x in load(refs[:-1]):
        out[at] = x
        at += 1


def halve(a, b, keep, send):
    n = keep.shape[0]
    for i in range(n):
        keep[i] = a[i] + b[i]
        send[i] = a[n + i] + b[n + i]


def add_parts(a, b, *outs):
    for i, out in enumerate(outs):
        out[0] = a[i] + b[i]


def exchange(v, hi, lo):
    n1 = trade(v, "col", 1)
    (c1,) = glue(join, [v, n1], 2)
    n2 = trade(c1, "col", 3)
    t0, t1 = turned_of([c1, n2], hi, lo, (4, 4), (0, 1, 3, 2), (0, 2, 4, 6, 1, 3, 5, 7))
    x1 = trade(v, "row", 2)
    (s1,) = glue(join, [v, x1], 2)
    z1 = trade(s1, "row", 1)
    (s2,) = glue(join, [s1, z1], 4)
    z2 = trade(s2, "row", 4)
    p0, p1 = plain_of([s2, z2], hi, lo, (2, 2), (0, 2, 1, 3, 4, 6, 5, 7), (0, 1, 3, 2))
    u0, u2, u4, u6 = glue(add_parts, [t0, trade(t1, "row", 1)], 1, 1, 1, 1)
    w = u0 + trade(u2, "row", 2) + trade(u4, "row", 4) + trade(u6, "row", 6)
    q0 = trade(p1, "col", 3)
    g0, g1 = glue(halve, [p0, q0], 1, 1)
    last = trade(g1, "col", 1)
    return (g0 + last + w)[0]


def solution(mesh):
    sizes = mesh.shape

    def per_device(vectors, values, block_rows, block_cols, counts):
        blk = math.isqrt(values.shape[1])
        piece = vectors.shape[1]
        nbr, nbc = sizes["col"] * piece // blk, sizes["row"] * piece // blk
        fits = nbr * nbc * blk * blk * 4 <= DENSE_LIMIT
        square = sizes["row"] == 8 and sizes["col"] == 4
        if not (fits and square and piece == LANES and 2 * blk == LANES and values.shape[0] % SUB == 0):
            return by_blocks(blk, vectors, values, block_rows, block_cols, counts)
        _, hi, lo = build(blk, nbr, nbc, vectors, values, block_rows, block_cols, counts)
        return exchange(vectors, hi, lo)

    spec = P("row", "col")
    return jax.shard_map(
        per_device,
        mesh=mesh,
        in_specs=(P(None, ("row", "col")), spec, spec, spec, spec),
        out_specs=P(None, ("row", "col")),
        check_vma=False,
    )
```

```python
import functools
import math

import jax
import jax.numpy as jnp
from jax import lax
from jax.experimental import pallas as pl
from jax.experimental.pallas import tpu as pltpu
from jax.sharding import PartitionSpec as P

LANES = 128
SUB = 8
DENSE_LIMIT = 4 << 20
f32, bf16 = jnp.float32, jnp.bfloat16
VMEM = pl.BlockSpec(memory_space=pltpu.VMEM)
SMEM = pl.BlockSpec(memory_space=pltpu.SMEM)
NT = (((1,), (1,)), ((), ()))


def tile_terms(blocks, rows, cols, count, row_seg, col_seg):
    highest = lax.Precision.HIGHEST
    slots = blocks.shape[0]
    nvec = row_seg.shape[0]
    row_blocks = row_seg.shape[1] // blocks.shape[1]
    col_blocks = col_seg.shape[1] // blocks.shape[1]
    width = blocks.shape[1]
    live = (jnp.arange(slots, dtype=jnp.int32) < count).astype(jnp.float32)
    row_hits = (rows[:, None] == jnp.arange(row_blocks, dtype=jnp.int32)[None, :]).astype(jnp.float32) * live[:, None]
    col_hits = (cols[:, None] == jnp.arange(col_blocks, dtype=jnp.int32)[None, :]).astype(jnp.float32) * live[:, None]
    row_parts = row_seg.reshape(nvec, row_blocks, width)
    col_parts = col_seg.reshape(nvec, col_blocks, width)
    col_pick = jnp.take(col_parts, cols, axis=1)
    row_pick = jnp.take(row_parts, rows, axis=1)
    plain = jnp.einsum("kij,vkj->vki", blocks, col_pick, precision=highest)
    turned = jnp.einsum("kji,vkj->vki", blocks, row_pick, precision=highest)
    plain_part = jnp.einsum("kb,vki->vbi", row_hits, plain, precision=highest).reshape(nvec, row_blocks * width)
    turned_part = jnp.einsum("kb,vki->vbi", col_hits, turned, precision=highest).reshape(nvec, col_blocks * width)
    return plain_part, turned_part


def by_blocks(blk, vectors, values, block_rows, block_cols, counts):
    row_seg = lax.all_gather(vectors, "col", axis=1, tiled=True)
    col_seg = lax.all_gather(vectors, "row", axis=1, tiled=True)
    blocks = values.reshape(values.shape[0], blk, blk)
    plain, turned = tile_terms(blocks, block_rows[0], block_cols[0], counts[0, 0], row_seg, col_seg)
    plain = lax.psum_scatter(plain, "col", scatter_dimension=1, tiled=True)
    turned = lax.psum_scatter(turned, "row", scatter_dimension=1, tiled=True)
    return plain + turned


def init_kernel(acc):
    acc[...] = jnp.zeros_like(acc)


def count_kernel(count, used):
    used[...] = jnp.full(used.shape, count[0, 0], used.dtype)


def build_kernel(blk, values, rows, cols, count, start, hi, lo, acc):
    del start
    r, c = lax.axis_index("row"), lax.axis_index("col")
    half = blk // 2
    steps = half // SUB
    group = half * SUB
    used = count[...]
    side = lax.broadcasted_iota(jnp.int32, (SUB, LANES), 1) // blk

    def add_slot(k, first):
        br = rows[0, k] ^ (c * 2)
        bc = cols[0, k] ^ (r * 2)
        q, odd = bc // 2, bc % 2
        keep = (side == odd) & (used > k)
        swapped = jnp.broadcast_to(odd, (SUB, LANES)) == 1
        for s in range(steps):
            two = values[pl.ds(first + s * SUB * SUB, SUB, stride=SUB), :]
            turn = swap(two)
            at = br * blk + 2 * SUB * s
            acc[q, pl.ds(at, SUB, stride=2), :] += jnp.where(keep, jnp.where(swapped, turn, two), 0.0)
            acc[q, pl.ds(at + 1, SUB, stride=2), :] += jnp.where(keep, jnp.where(swapped, two, turn), 0.0)

    for k in range(values.shape[0] // half):
        add_slot(k, k // SUB * group + k % SUB)
    for q in range(acc.shape[0]):
        dense = acc[q]
        top = dense.astype(bf16)
        hi[q] = top
        lo[q] = (dense - top.astype(f32)).astype(bf16)


def build(blk, nbr, nbc, vectors, values, block_rows, block_cols, counts):
    slots = values.shape[0]
    half = blk // 2
    view = values.reshape(slots // SUB, SUB, half, LANES).transpose(0, 2, 1, 3).reshape(slots * half, LANES)
    shape = (nbc // 2, nbr * blk, LANES)
    start = pl.pallas_call(
        init_kernel,
        out_shape=jax.ShapeDtypeStruct(shape, f32),
        out_specs=VMEM,
        compiler_params=pltpu.CompilerParams(vmem_limit_bytes=4 << 20),
        cost_estimate=pl.CostEstimate(flops=1 << 20, bytes_accessed=2 << 20, transcendentals=0),
        name="init",
    )()
    used = pl.pallas_call(
        count_kernel,
        out_shape=jax.ShapeDtypeStruct((SUB, LANES), jnp.int32),
        in_specs=[SMEM],
        out_specs=VMEM,
        compiler_params=pltpu.CompilerParams(vmem_limit_bytes=1 << 20),
        name="count",
    )(counts)
    hi, lo, _ = pl.pallas_call(
        functools.partial(build_kernel, blk),
        out_shape=[jax.ShapeDtypeStruct(shape, bf16)] * 2 + [jax.ShapeDtypeStruct(shape, f32)],
        in_specs=[VMEM, SMEM, SMEM, VMEM, VMEM],
        out_specs=[VMEM] * 3,
        input_output_aliases={4: 2},
        compiler_params=pltpu.CompilerParams(vmem_limit_bytes=12 << 20),
        cost_estimate=pl.CostEstimate(flops=1 << 20, bytes_accessed=6 << 20, transcendentals=0),
        name="build",
    )(view, block_rows, block_cols, used, start)
    return vectors, hi, lo


def split(x):
    top = x.astype(bf16).astype(f32)
    return jnp.concatenate([top, x - top], 0)


def swap(x):
    return pltpu.roll(x, LANES // 2, 1)


def wide(ref, q):
    return jnp.concatenate([ref[q], ref[q + 1]], 1)


def load(refs):
    out = []
    for ref in refs:
        if len(ref.shape) == 2:
            out.append(ref[...])
        else:
            out += [ref[i] for i in range(ref.shape[0])]
    return out


def pieces(refs, names):
    return dict(zip(names, load(refs), strict=True))


def places(refs, names):
    return dict(zip(names, ((ref, i) for ref in refs for i in range(ref.shape[0])), strict=True))


def turned_kernel(nx, take, put, *refs):
    xs, (hi, lo), outs = pieces(refs[:nx], take), refs[nx : nx + 2], places(refs[nx + 2 :], put)
    nv = xs[0].shape[0]
    left = jnp.concatenate([split(xs[k]) for k in range(len(xs))], 1).astype(bf16)
    for q in range(0, len(outs), 2):
        t = jnp.dot(left, wide(hi, q), preferred_element_type=f32) + jnp.dot(left, wide(lo, q), preferred_element_type=f32)
        t = t[:nv] + t[nv:]
        for i in range(2):
            out, at = outs[q + i]
            out[at] = t[:, LANES * i : LANES * (i + 1)]


def plain_kernel(nx, take, put, *refs):
    xs, (hi, lo), outs = pieces(refs[:nx], take), refs[nx : nx + 2], places(refs[nx + 2 :], put)
    nv = xs[0].shape[0]
    total = 0.0
    for q in range(0, len(xs), 2):
        left = jnp.concatenate([split(xs[q]), split(xs[q + 1])], 1).astype(bf16)
        for part in (hi, lo):
            total += lax.dot_general(left, wide(part, q), NT, preferred_element_type=f32)
    total = total[:nv] + total[nv:]
    for k, (out, at) in outs.items():
        out[at] = total[:, LANES * k : LANES * (k + 1)]


def call(kernel, xs, hi, lo, outs, take, put):
    nv = xs[0].shape[-2]
    return pl.pallas_call(
        functools.partial(kernel, len(xs), take, put),
        out_shape=[jax.ShapeDtypeStruct((n, nv, LANES), f32) for n in outs],
        in_specs=[VMEM] * (len(xs) + 2),
        out_specs=[VMEM] * len(outs),
        compiler_params=pltpu.CompilerParams(vmem_limit_bytes=12 << 20),
        cost_estimate=pl.CostEstimate(flops=1 << 26, bytes_accessed=2 << 20, transcendentals=0),
    )(*xs, hi, lo)


def turned_of(xs, hi, lo, outs, take, put):
    return call(turned_kernel, xs, hi, lo, outs, take, put)


def plain_of(xs, hi, lo, outs, take, put):
    return call(plain_kernel, xs, hi, lo, outs, take, put)


def trade(x, axis, step):
    n = lax.axis_size(axis)
    return lax.ppermute(x, axis, [(i, i ^ step) for i in range(n)])


def glue(body, ins, *outs):
    return pl.pallas_call(
        body,
        out_shape=[jax.ShapeDtypeStruct((n,) + ins[0].shape[-2:], f32) for n in outs],
        in_specs=[VMEM] * len(ins),
        out_specs=[VMEM] * len(outs),
        compiler_params=pltpu.CompilerParams(vmem_limit_bytes=1 << 20),
    )(*ins)


def join(*refs):
    out, at = refs[-1], 0
    for x in load(refs[:-1]):
        out[at] = x
        at += 1


def halve(a, b, keep, send):
    n = keep.shape[0]
    for i in range(n):
        keep[i] = a[i] + b[i]
        send[i] = a[n + i] + b[n + i]


def add_parts(a, b, *outs):
    for i, out in enumerate(outs):
        out[0] = a[i] + b[i]


def exchange(v, hi, lo):
    n1 = trade(v, "col", 1)
    (c1,) = glue(join, [v, n1], 2)
    n2 = trade(c1, "col", 3)
    t0, t1 = turned_of([c1, n2], hi, lo, (4, 4), (0, 1, 3, 2), (0, 2, 4, 6, 1, 3, 5, 7))
    x1 = trade(v, "row", 2)
    (s1,) = glue(join, [v, x1], 2)
    z1 = trade(s1, "row", 1)
    (s2,) = glue(join, [s1, z1], 4)
    z2 = trade(s2, "row", 4)
    p0, p1 = plain_of([s2, z2], hi, lo, (2, 2), (0, 2, 1, 3, 4, 6, 5, 7), (0, 1, 3, 2))
    u0, u2, u4, u6 = glue(add_parts, [t0, trade(t1, "row", 1)], 1, 1, 1, 1)
    w = u0 + trade(u2, "row", 2) + trade(u4, "row", 4) + trade(u6, "row", 6)
    q0 = trade(p1, "col", 3)
    g0, g1 = glue(halve, [p0, q0], 1, 1)
    last = trade(g1, "col", 1)
    return (g0 + last + w)[0]


def solution(mesh):
    sizes = mesh.shape

    def per_device(vectors, values, block_rows, block_cols, counts):
        blk = math.isqrt(values.shape[1])
        piece = vectors.shape[1]
        nbr, nbc = sizes["col"] * piece // blk, sizes["row"] * piece // blk
        fits = nbr * nbc * blk * blk * 4 <= DENSE_LIMIT
        square = sizes["row"] == 8 and sizes["col"] == 4
        if not (fits and square and piece == LANES and 2 * blk == LANES and values.shape[0] % SUB == 0):
            return by_blocks(blk, vectors, values, block_rows, block_cols, counts)
        _, hi, lo = build(blk, nbr, nbc, vectors, values, block_rows, block_cols, counts)
        return exchange(vectors, hi, lo)

    spec = P("row", "col")
    return jax.shard_map(
        per_device,
        mesh=mesh,
        in_specs=(P(None, ("row", "col")), spec, spec, spec, spec),
        out_specs=P(None, ("row", "col")),
        check_vma=False,
    )
```

```python
import functools
import math

import jax
import jax.numpy as jnp
from jax import lax
from jax.experimental import pallas as pl
from jax.experimental.pallas import tpu as pltpu
from jax.sharding import PartitionSpec as P

LANES = 128
SUB = 8
DENSE_LIMIT = 4 << 20
f32, bf16 = jnp.float32, jnp.bfloat16
VMEM = pl.BlockSpec(memory_space=pltpu.VMEM)
SMEM = pl.BlockSpec(memory_space=pltpu.SMEM)
NT = (((1,), (1,)), ((), ()))


def tile_terms(blocks, rows, cols, count, row_seg, col_seg):
    highest = lax.Precision.HIGHEST
    slots = blocks.shape[0]
    nvec = row_seg.shape[0]
    row_blocks = row_seg.shape[1] // blocks.shape[1]
    col_blocks = col_seg.shape[1] // blocks.shape[1]
    width = blocks.shape[1]
    live = (jnp.arange(slots, dtype=jnp.int32) < count).astype(jnp.float32)
    row_hits = (rows[:, None] == jnp.arange(row_blocks, dtype=jnp.int32)[None, :]).astype(jnp.float32) * live[:, None]
    col_hits = (cols[:, None] == jnp.arange(col_blocks, dtype=jnp.int32)[None, :]).astype(jnp.float32) * live[:, None]
    row_parts = row_seg.reshape(nvec, row_blocks, width)
    col_parts = col_seg.reshape(nvec, col_blocks, width)
    col_pick = jnp.take(col_parts, cols, axis=1)
    row_pick = jnp.take(row_parts, rows, axis=1)
    plain = jnp.einsum("kij,vkj->vki", blocks, col_pick, precision=highest)
    turned = jnp.einsum("kji,vkj->vki", blocks, row_pick, precision=highest)
    plain_part = jnp.einsum("kb,vki->vbi", row_hits, plain, precision=highest).reshape(nvec, row_blocks * width)
    turned_part = jnp.einsum("kb,vki->vbi", col_hits, turned, precision=highest).reshape(nvec, col_blocks * width)
    return plain_part, turned_part


def by_blocks(blk, vectors, values, block_rows, block_cols, counts):
    row_seg = lax.all_gather(vectors, "col", axis=1, tiled=True)
    col_seg = lax.all_gather(vectors, "row", axis=1, tiled=True)
    blocks = values.reshape(values.shape[0], blk, blk)
    plain, turned = tile_terms(blocks, block_rows[0], block_cols[0], counts[0, 0], row_seg, col_seg)
    plain = lax.psum_scatter(plain, "col", scatter_dimension=1, tiled=True)
    turned = lax.psum_scatter(turned, "row", scatter_dimension=1, tiled=True)
    return plain + turned


def init_kernel(acc):
    acc[...] = jnp.zeros_like(acc)


def count_kernel(count, used):
    used[...] = jnp.full(used.shape, count[0, 0], used.dtype)


def build_kernel(blk, values, rows, cols, count, start, hi, lo, acc):
    del start
    r, c = lax.axis_index("row"), lax.axis_index("col")
    half = blk // 2
    steps = half // SUB
    group = half * SUB
    used = count[...]
    span = 2 * (acc.shape[1] // blk)
    codes = (cols[...] ^ (r * 2)) * (span // 2) + (rows[...] ^ (c * 2))
    side = lax.broadcasted_iota(jnp.int32, (SUB, LANES), 1) // blk

    def add_slot(k, first):
        code = codes[0, k]
        q, odd, base = code // span, code // (span // 2) % 2, code % (span // 2) * blk
        keep = (side == odd) & (used > k)
        swapped = jnp.broadcast_to(odd, (SUB, LANES)) == 1
        for s in range(steps):
            two = values[pl.ds(first + s * SUB * SUB, SUB, stride=SUB), :]
            turn = swap(two)
            at = base + 2 * SUB * s
            acc[q, pl.ds(at, SUB, stride=2), :] += jnp.where(keep, jnp.where(swapped, turn, two), 0.0)
            acc[q, pl.ds(at + 1, SUB, stride=2), :] += jnp.where(keep, jnp.where(swapped, two, turn), 0.0)

    for k in range(values.shape[0] // half):
        add_slot(k, k // SUB * group + k % SUB)
    for q in range(acc.shape[0]):
        dense = acc[q]
        top = dense.astype(bf16)
        hi[q] = top
        lo[q] = (dense - top.astype(f32)).astype(bf16)


def build(blk, nbr, nbc, vectors, values, block_rows, block_cols, counts):
    slots = values.shape[0]
    half = blk // 2
    view = values.reshape(slots // SUB, SUB, half, LANES).transpose(0, 2, 1, 3).reshape(slots * half, LANES)
    shape = (nbc // 2, nbr * blk, LANES)
    start = pl.pallas_call(
        init_kernel,
        out_shape=jax.ShapeDtypeStruct(shape, f32),
        out_specs=VMEM,
        compiler_params=pltpu.CompilerParams(vmem_limit_bytes=4 << 20),
        cost_estimate=pl.CostEstimate(flops=1 << 20, bytes_accessed=2 << 20, transcendentals=0),
        name="init",
    )()
    used = pl.pallas_call(
        count_kernel,
        out_shape=jax.ShapeDtypeStruct((SUB, LANES), jnp.int32),
        in_specs=[SMEM],
        out_specs=VMEM,
        compiler_params=pltpu.CompilerParams(vmem_limit_bytes=1 << 20),
        name="count",
    )(counts)
    hi, lo, _ = pl.pallas_call(
        functools.partial(build_kernel, blk),
        out_shape=[jax.ShapeDtypeStruct(shape, bf16)] * 2 + [jax.ShapeDtypeStruct(shape, f32)],
        in_specs=[VMEM] * 5,
        out_specs=[VMEM] * 3,
        input_output_aliases={4: 2},
        compiler_params=pltpu.CompilerParams(vmem_limit_bytes=12 << 20),
        cost_estimate=pl.CostEstimate(flops=1 << 20, bytes_accessed=6 << 20, transcendentals=0),
        name="build",
    )(view, block_rows, block_cols, used, start)
    return vectors, hi, lo


def split(x):
    top = x.astype(bf16).astype(f32)
    return jnp.concatenate([top, x - top], 0)


def swap(x):
    return pltpu.roll(x, LANES // 2, 1)


def wide(ref, q):
    return jnp.concatenate([ref[q], ref[q + 1]], 1)


def load(refs):
    out = []
    for ref in refs:
        if len(ref.shape) == 2:
            out.append(ref[...])
        else:
            out += [ref[i] for i in range(ref.shape[0])]
    return out


def pieces(refs, names):
    return dict(zip(names, load(refs), strict=True))


def places(refs, names):
    return dict(zip(names, ((ref, i) for ref in refs for i in range(ref.shape[0])), strict=True))


def turned_kernel(nx, take, put, *refs):
    xs, (hi, lo), outs = pieces(refs[:nx], take), refs[nx : nx + 2], places(refs[nx + 2 :], put)
    nv = xs[0].shape[0]
    left = jnp.concatenate([split(xs[k]) for k in range(len(xs))], 1).astype(bf16)
    for q in range(0, len(outs), 2):
        t = jnp.dot(left, wide(hi, q), preferred_element_type=f32) + jnp.dot(left, wide(lo, q), preferred_element_type=f32)
        t = t[:nv] + t[nv:]
        for i in range(2):
            out, at = outs[q + i]
            out[at] = t[:, LANES * i : LANES * (i + 1)]


def plain_kernel(nx, take, put, *refs):
    xs, (hi, lo), outs = pieces(refs[:nx], take), refs[nx : nx + 2], places(refs[nx + 2 :], put)
    nv = xs[0].shape[0]
    total = 0.0
    for q in range(0, len(xs), 2):
        left = jnp.concatenate([split(xs[q]), split(xs[q + 1])], 1).astype(bf16)
        for part in (hi, lo):
            total += lax.dot_general(left, wide(part, q), NT, preferred_element_type=f32)
    total = total[:nv] + total[nv:]
    for k, (out, at) in outs.items():
        out[at] = total[:, LANES * k : LANES * (k + 1)]


def call(kernel, xs, hi, lo, outs, take, put):
    nv = xs[0].shape[-2]
    return pl.pallas_call(
        functools.partial(kernel, len(xs), take, put),
        out_shape=[jax.ShapeDtypeStruct((n, nv, LANES), f32) for n in outs],
        in_specs=[VMEM] * (len(xs) + 2),
        out_specs=[VMEM] * len(outs),
        compiler_params=pltpu.CompilerParams(vmem_limit_bytes=12 << 20),
        cost_estimate=pl.CostEstimate(flops=1 << 26, bytes_accessed=2 << 20, transcendentals=0),
    )(*xs, hi, lo)


def turned_of(xs, hi, lo, outs, take, put):
    return call(turned_kernel, xs, hi, lo, outs, take, put)


def plain_of(xs, hi, lo, outs, take, put):
    return call(plain_kernel, xs, hi, lo, outs, take, put)


def trade(x, axis, step):
    n = lax.axis_size(axis)
    return lax.ppermute(x, axis, [(i, i ^ step) for i in range(n)])


def glue(body, ins, *outs):
    return pl.pallas_call(
        body,
        out_shape=[jax.ShapeDtypeStruct((n,) + ins[0].shape[-2:], f32) for n in outs],
        in_specs=[VMEM] * len(ins),
        out_specs=[VMEM] * len(outs),
        compiler_params=pltpu.CompilerParams(vmem_limit_bytes=1 << 20),
    )(*ins)


def join(*refs):
    out, at = refs[-1], 0
    for x in load(refs[:-1]):
        out[at] = x
        at += 1


def halve(a, b, keep, send):
    n = keep.shape[0]
    for i in range(n):
        keep[i] = a[i] + b[i]
        send[i] = a[n + i] + b[n + i]


def add_parts(a, b, *outs):
    for i, out in enumerate(outs):
        out[0] = a[i] + b[i]


def exchange(v, hi, lo):
    n1 = trade(v, "col", 1)
    (c1,) = glue(join, [v, n1], 2)
    n2 = trade(c1, "col", 3)
    t0, t1 = turned_of([c1, n2], hi, lo, (4, 4), (0, 1, 3, 2), (0, 2, 4, 6, 1, 3, 5, 7))
    x1 = trade(v, "row", 2)
    (s1,) = glue(join, [v, x1], 2)
    z1 = trade(s1, "row", 1)
    (s2,) = glue(join, [s1, z1], 4)
    z2 = trade(s2, "row", 4)
    p0, p1 = plain_of([s2, z2], hi, lo, (2, 2), (0, 2, 1, 3, 4, 6, 5, 7), (0, 1, 3, 2))
    u0, u2, u4, u6 = glue(add_parts, [t0, trade(t1, "row", 1)], 1, 1, 1, 1)
    w = u0 + trade(u2, "row", 2) + trade(u4, "row", 4) + trade(u6, "row", 6)
    q0 = trade(p1, "col", 3)
    g0, g1 = glue(halve, [p0, q0], 1, 1)
    last = trade(g1, "col", 1)
    return (g0 + last + w)[0]


def solution(mesh):
    sizes = mesh.shape

    def per_device(vectors, values, block_rows, block_cols, counts):
        blk = math.isqrt(values.shape[1])
        piece = vectors.shape[1]
        nbr, nbc = sizes["col"] * piece // blk, sizes["row"] * piece // blk
        fits = nbr * nbc * blk * blk * 4 <= DENSE_LIMIT
        square = sizes["row"] == 8 and sizes["col"] == 4
        if not (fits and square and piece == LANES and 2 * blk == LANES and values.shape[0] % SUB == 0):
            return by_blocks(blk, vectors, values, block_rows, block_cols, counts)
        _, hi, lo = build(blk, nbr, nbc, vectors, values, block_rows, block_cols, counts)
        return exchange(vectors, hi, lo)

    spec = P("row", "col")
    return jax.shard_map(
        per_device,
        mesh=mesh,
        in_specs=(P(None, ("row", "col")), spec, spec, spec, spec),
        out_specs=P(None, ("row", "col")),
        check_vma=False,
    )
```

```python
import functools
import math

import jax
import jax.numpy as jnp
from jax import lax
from jax.experimental import pallas as pl
from jax.experimental.pallas import tpu as pltpu
from jax.sharding import PartitionSpec as P

LANES = 128
SUB = 8
DENSE_LIMIT = 4 << 20
f32, bf16 = jnp.float32, jnp.bfloat16
VMEM = pl.BlockSpec(memory_space=pltpu.VMEM)
SMEM = pl.BlockSpec(memory_space=pltpu.SMEM)
NT = (((1,), (1,)), ((), ()))


def tile_terms(blocks, rows, cols, count, row_seg, col_seg):
    highest = lax.Precision.HIGHEST
    slots = blocks.shape[0]
    nvec = row_seg.shape[0]
    row_blocks = row_seg.shape[1] // blocks.shape[1]
    col_blocks = col_seg.shape[1] // blocks.shape[1]
    width = blocks.shape[1]
    live = (jnp.arange(slots, dtype=jnp.int32) < count).astype(jnp.float32)
    row_hits = (rows[:, None] == jnp.arange(row_blocks, dtype=jnp.int32)[None, :]).astype(jnp.float32) * live[:, None]
    col_hits = (cols[:, None] == jnp.arange(col_blocks, dtype=jnp.int32)[None, :]).astype(jnp.float32) * live[:, None]
    row_parts = row_seg.reshape(nvec, row_blocks, width)
    col_parts = col_seg.reshape(nvec, col_blocks, width)
    col_pick = jnp.take(col_parts, cols, axis=1)
    row_pick = jnp.take(row_parts, rows, axis=1)
    plain = jnp.einsum("kij,vkj->vki", blocks, col_pick, precision=highest)
    turned = jnp.einsum("kji,vkj->vki", blocks, row_pick, precision=highest)
    plain_part = jnp.einsum("kb,vki->vbi", row_hits, plain, precision=highest).reshape(nvec, row_blocks * width)
    turned_part = jnp.einsum("kb,vki->vbi", col_hits, turned, precision=highest).reshape(nvec, col_blocks * width)
    return plain_part, turned_part


def by_blocks(blk, vectors, values, block_rows, block_cols, counts):
    row_seg = lax.all_gather(vectors, "col", axis=1, tiled=True)
    col_seg = lax.all_gather(vectors, "row", axis=1, tiled=True)
    blocks = values.reshape(values.shape[0], blk, blk)
    plain, turned = tile_terms(blocks, block_rows[0], block_cols[0], counts[0, 0], row_seg, col_seg)
    plain = lax.psum_scatter(plain, "col", scatter_dimension=1, tiled=True)
    turned = lax.psum_scatter(turned, "row", scatter_dimension=1, tiled=True)
    return plain + turned


def init_kernel(acc):
    acc[...] = jnp.zeros_like(acc)


def count_kernel(count, used):
    used[...] = jnp.full(used.shape, count[0, 0], used.dtype)


def build_kernel(blk, values, rows, cols, count, start, hi, lo, acc):
    del start
    r, c = lax.axis_index("row"), lax.axis_index("col")
    half = blk // 2
    steps = half // SUB
    group = half * SUB
    used = count[...]
    span = 2 * (acc.shape[1] // blk)
    codes = (cols[...] ^ (r * 2)) * (span // 2) + (rows[...] ^ (c * 2))
    side = lax.broadcasted_iota(jnp.int32, (SUB, LANES), 1) // blk

    def add_slot(k, first):
        code = codes[0, k]
        q, odd, base = code // span, code // (span // 2) % 2, code % (span // 2) * blk
        keep = (side == odd) & (used > k)
        swapped = jnp.broadcast_to(odd, (SUB, LANES)) == 1
        for s in range(steps):
            two = values[pl.ds(first + s * SUB * SUB, SUB, stride=SUB), :]
            turn = swap(two)
            at = base + 2 * SUB * s
            acc[q, pl.ds(at, SUB, stride=2), :] += jnp.where(keep, jnp.where(swapped, turn, two), 0.0)
            acc[q, pl.ds(at + 1, SUB, stride=2), :] += jnp.where(keep, jnp.where(swapped, two, turn), 0.0)

    for k in range(values.shape[0] // half):
        add_slot(k, k // SUB * group + k % SUB)
    for q in range(acc.shape[0]):
        dense = acc[q]
        top = dense.astype(bf16)
        hi[q] = top
        lo[q] = (dense - top.astype(f32)).astype(bf16)


def build(blk, nbr, nbc, vectors, values, block_rows, block_cols, counts):
    slots = values.shape[0]
    half = blk // 2
    view = values.reshape(slots // SUB, SUB, half, LANES).transpose(0, 2, 1, 3).reshape(slots * half, LANES)
    shape = (nbc // 2, nbr * blk, LANES)
    start = pl.pallas_call(
        init_kernel,
        out_shape=jax.ShapeDtypeStruct(shape, f32),
        out_specs=VMEM,
        compiler_params=pltpu.CompilerParams(vmem_limit_bytes=4 << 20),
        cost_estimate=pl.CostEstimate(flops=1 << 20, bytes_accessed=2 << 20, transcendentals=0),
        name="init",
    )()
    used = pl.pallas_call(
        count_kernel,
        out_shape=jax.ShapeDtypeStruct((SUB, LANES), jnp.int32),
        in_specs=[SMEM],
        out_specs=VMEM,
        compiler_params=pltpu.CompilerParams(vmem_limit_bytes=1 << 20),
        name="count",
    )(counts)
    hi, lo, _ = pl.pallas_call(
        functools.partial(build_kernel, blk),
        out_shape=[jax.ShapeDtypeStruct(shape, bf16)] * 2 + [jax.ShapeDtypeStruct(shape, f32)],
        in_specs=[VMEM] * 5,
        out_specs=[VMEM] * 3,
        input_output_aliases={4: 2},
        compiler_params=pltpu.CompilerParams(vmem_limit_bytes=12 << 20),
        cost_estimate=pl.CostEstimate(flops=1 << 20, bytes_accessed=6 << 20, transcendentals=0),
        name="build",
    )(view, block_rows, block_cols, used, start)
    return vectors, hi, lo


def split(x):
    top = x.astype(bf16).astype(f32)
    return jnp.concatenate([top, x - top], 0)


def swap(x):
    return pltpu.roll(x, LANES // 2, 1)


def load(refs):
    out = []
    for ref in refs:
        if len(ref.shape) == 2:
            out.append(ref[...])
        else:
            out += [ref[i] for i in range(ref.shape[0])]
    return out


def pieces(refs, names):
    return dict(zip(names, load(refs), strict=True))


def places(refs, names):
    return dict(zip(names, ((ref, i) for ref in refs for i in range(ref.shape[0])), strict=True))


def turned_kernel(nx, take, put, *refs):
    xs, (hi, lo), outs = pieces(refs[:nx], take), refs[nx : nx + 2], places(refs[nx + 2 :], put)
    nv = xs[0].shape[0]
    left = jnp.concatenate([split(xs[k]) for k in range(len(xs))], 1).astype(bf16)
    for pair in zip(put[::2], put[1::2]):
        t = 0.0
        for part in (hi, lo):
            t += jnp.dot(left, jnp.concatenate([part[q] for q in pair], 1), preferred_element_type=f32)
        t = t[:nv] + t[nv:]
        for i, q in enumerate(pair):
            out, at = outs[q]
            out[at] = t[:, LANES * i : LANES * (i + 1)]


def plain_kernel(nx, take, put, *refs):
    xs, (hi, lo), outs = pieces(refs[:nx], take), refs[nx : nx + 2], places(refs[nx + 2 :], put)
    nv = xs[0].shape[0]
    first = min(put)
    rows = slice(LANES * first, LANES * (max(put) + 1))
    total = 0.0
    for q in range(0, len(xs), 2):
        left = jnp.concatenate([split(xs[q]), split(xs[q + 1])], 1).astype(bf16)
        for part in (hi, lo):
            right = jnp.concatenate([part[q, rows, :], part[q + 1, rows, :]], 1)
            total += lax.dot_general(left, right, NT, preferred_element_type=f32)
    total = total[:nv] + total[nv:]
    for k, (out, at) in outs.items():
        out[at] = total[:, LANES * (k - first) : LANES * (k - first + 1)]


def call(kernel, xs, hi, lo, outs, take, put):
    nv = xs[0].shape[-2]
    return pl.pallas_call(
        functools.partial(kernel, len(xs), take, put),
        out_shape=[jax.ShapeDtypeStruct((n, nv, LANES), f32) for n in outs],
        in_specs=[VMEM] * (len(xs) + 2),
        out_specs=[VMEM] * len(outs),
        compiler_params=pltpu.CompilerParams(vmem_limit_bytes=12 << 20),
        cost_estimate=pl.CostEstimate(flops=1 << 26, bytes_accessed=2 << 20, transcendentals=0),
    )(*xs, hi, lo)


def turned_of(xs, hi, lo, take, put):
    return call(turned_kernel, xs, hi, lo, (len(put),), take, put)[0]


def plain_of(xs, hi, lo, take, put):
    return call(plain_kernel, xs, hi, lo, (len(put),), take, put)[0]


def trade(x, axis, step):
    n = lax.axis_size(axis)
    return lax.ppermute(x, axis, [(i, i ^ step) for i in range(n)])


def glue(body, ins, *outs):
    return pl.pallas_call(
        body,
        out_shape=[jax.ShapeDtypeStruct((n,) + ins[0].shape[-2:], f32) for n in outs],
        in_specs=[VMEM] * len(ins),
        out_specs=[VMEM] * len(outs),
        compiler_params=pltpu.CompilerParams(vmem_limit_bytes=1 << 20),
    )(*ins)


def join(*refs):
    out, at = refs[-1], 0
    for x in load(refs[:-1]):
        out[at] = x
        at += 1


def halve(a, b, keep, send):
    n = keep.shape[0]
    for i in range(n):
        keep[i] = a[i] + b[i]
        send[i] = a[n + i] + b[n + i]


def add_parts(a, b, *outs):
    for i, out in enumerate(outs):
        out[0] = a[i] + b[i]


def exchange(v, hi, lo):
    n1 = trade(v, "col", 1)
    (c1,) = glue(join, [v, n1], 2)
    n2 = trade(c1, "col", 3)
    sent = turned_of([c1, n2], hi, lo, (0, 1, 3, 2), (1, 3, 5, 7))
    kept = turned_of([c1, n2], hi, lo, (0, 1, 3, 2), (0, 2, 4, 6))
    x1 = trade(v, "row", 2)
    (s1,) = glue(join, [v, x1], 2)
    z1 = trade(s1, "row", 1)
    (s2,) = glue(join, [s1, z1], 4)
    z2 = trade(s2, "row", 4)
    u0, u2, u4, u6 = glue(add_parts, [kept, trade(sent, "row", 1)], 1, 1, 1, 1)
    w = u0 + trade(u2, "row", 2) + trade(u4, "row", 4) + trade(u6, "row", 6)
    p1 = plain_of([s2, z2], hi, lo, (0, 2, 1, 3, 4, 6, 5, 7), (3, 2))
    p0 = plain_of([s2, z2], hi, lo, (0, 2, 1, 3, 4, 6, 5, 7), (0, 1))
    q0 = trade(p1, "col", 3)
    g0, g1 = glue(halve, [p0, q0], 1, 1)
    last = trade(g1, "col", 1)
    return (g0 + last + w)[0]


def solution(mesh):
    sizes = mesh.shape

    def per_device(vectors, values, block_rows, block_cols, counts):
        blk = math.isqrt(values.shape[1])
        piece = vectors.shape[1]
        nbr, nbc = sizes["col"] * piece // blk, sizes["row"] * piece // blk
        fits = nbr * nbc * blk * blk * 4 <= DENSE_LIMIT
        square = sizes["row"] == 8 and sizes["col"] == 4
        if not (fits and square and piece == LANES and 2 * blk == LANES and values.shape[0] % SUB == 0):
            return by_blocks(blk, vectors, values, block_rows, block_cols, counts)
        _, hi, lo = build(blk, nbr, nbc, vectors, values, block_rows, block_cols, counts)
        return exchange(vectors, hi, lo)

    spec = P("row", "col")
    return jax.shard_map(
        per_device,
        mesh=mesh,
        in_specs=(P(None, ("row", "col")), spec, spec, spec, spec),
        out_specs=P(None, ("row", "col")),
        check_vma=False,
    )
```
